1024 devices in a mesh: slab: 16 (over x_hi, y), sample: 64 (over z, x_lo, core).
Axes of the slice: x: 8 (x_hi: 2, x_lo: 4; x = x_hi * 4 + x_lo), y: 8, z: 8, core: 2. Of those that a mesh axis runs over, the one named last changes fastest.
Arguments:
- activations: bfloat16 [64, 32, 64, 8, 128], P('sample', None, 'slab'), may hold values from -6 to 6
- grad_out: bfloat16 [64, 64, 64, 8, 128], P('sample', 'slab'), may hold values from -6 to 6
- weight: bfloat16 [27, 64, 32], replicated, may hold values from -0.21875 to 0.21875
Outputs:
- grad_inputs: bfloat16 [64, 32, 64, 8, 128], P('sample', None, 'slab')
- grad_weight: float32 [27, 64, 32], replicated
- grad_bias: float32 [64], replicated
The draws below stay inside these ranges and needn't reach their ends.
All inputs are finite; a program needn't handle non-finite values.
Results may differ from the reference program's by a relative error of at most 0.001.
Values may be sent and summed in bfloat16 or wider, within the bound.
A program may use at most 32 MiB of HBM per device.

```python
import math
import jax
import jax.numpy as jnp
from jax import lax

CIN = 32
COUT = 64
NY = 8
NX = 128
SAMPLES = 64
NZ = 64


def shard_levels(own_key, shape, cuts, least, high):
    def one(dim, shards_of):
        draws = jax.random.uniform(jax.random.fold_in(jax.random.fold_in(own_key, 6), dim), (shards_of,), jnp.float32, least / len(cuts), high / len(cuts))
        return jnp.repeat(jnp.exp(draws), shape[dim] // shards_of).reshape((-1,) + (1,) * (len(shape) - dim - 1))

    gain = one(*cuts[0])
    for cut in cuts[1:]:
        gain = gain * one(*cut)
    return gain


def gaussian(stream_key, dims, scale, reach, split=(), kind=jnp.bfloat16):
    drawn = scale * jax.random.normal(stream_key, dims, jnp.float32)
    if split:
        drawn = drawn * shard_levels(stream_key, dims, split, -0.22, 0.18)
    return jnp.clip(drawn, -reach, reach).astype(kind)


def setup_inputs(seed: int = 0) -> dict:
    key_of = jax.random.split(jax.random.key(seed), 4)
    activations = gaussian(key_of[0], (SAMPLES, CIN, NZ, NY, NX), 1.0, 6.0, ((0, 64), (2, 16)))
    grad_out = gaussian(key_of[1], (SAMPLES, COUT, NZ, NY, NX), 1.0, 6.0, ((0, 64), (1, 16)))
    weight = gaussian(key_of[2], (27, COUT, CIN), (27 * CIN) ** -0.5, 0.21875)
    return dict(activations=activations, grad_out=grad_out, weight=weight)


def offsets_list():
    return [(shift_z, shift_y, shift_x) for shift_z in (-1, 0, 1) for shift_y in (-1, 0, 1) for shift_x in (-1, 0, 1)]

def one_sample(inputs, cotangent, weight):
    in_chan = inputs.shape[0]
    out_chan = cotangent.shape[0]
    planes, y_cells, x_cells = (inputs.shape[1], inputs.shape[2], inputs.shape[3])
    widths = ((0, 0), (1, 1), (1, 1), (1, 1))
    padded_in = jnp.pad(inputs, widths)
    padded_co = jnp.pad(cotangent, widths)
    center = cotangent.reshape(out_chan, -1)
    grad_in = jnp.zeros((in_chan, planes * y_cells * x_cells), jnp.float32)
    pieces = []
    for offset, (shift_z, shift_y, shift_x) in enumerate(offsets_list()):
        moved_in = padded_in[:, 1 + shift_z:1 + shift_z + planes, 1 + shift_y:1 + shift_y + y_cells, 1 + shift_x:1 + shift_x + x_cells].reshape(in_chan, -1)
        moved_co = padded_co[:, 1 - shift_z:1 - shift_z + planes, 1 - shift_y:1 - shift_y + y_cells, 1 - shift_x:1 - shift_x + x_cells].reshape(out_chan, -1)
        pieces.append(jnp.dot(center, moved_in.T, preferred_element_type=jnp.float32))
        grad_in = grad_in + jnp.dot(weight[offset].T, moved_co, preferred_element_type=jnp.float32)
    grad_in = grad_in.reshape(in_chan, planes, y_cells, x_cells).astype(jnp.bfloat16)
    return (grad_in, jnp.stack(pieces), lax.optimization_barrier(jnp.sum(center.astype(jnp.float32), axis=1)))

def reference(activations, grad_out, weight):

    def step(carry, pair):
        grad_in, wpart, bpart = one_sample(pair[0], pair[1], weight)
        return ((carry[0] + wpart, carry[1] + bpart), grad_in)
    start = (jnp.zeros((27, COUT, CIN), jnp.float32), jnp.zeros((COUT,), jnp.float32))
    totals, grad_inputs = lax.scan(step, start, (activations, grad_out))
    factor = 1.0 / math.sqrt(SAMPLES * NZ * NY * NX)
    return (grad_inputs, totals[0] * factor, totals[1] * factor)
```

```python
import functools
import math

import jax
import jax.numpy as jnp
from jax import lax
from jax.experimental import pallas as pl
from jax.experimental.pallas import tpu as pltpu
from jax.sharding import PartitionSpec as P

MESH = pl.DeviceIdType.MESH
F32 = jnp.float32
BF16 = jnp.bfloat16


def lane_shift(value, shift):
    lane = lax.broadcasted_iota(jnp.int32, value.shape, value.ndim - 1)
    rolled = pltpu.roll(value, shift % 128, value.ndim - 1)
    edge = 0 if shift > 0 else 127
    return jnp.where(lane == edge, 0.0, rolled)


def compute_kernel(g_ref, a_ref, w_ref, gi_ref, gw_ref, g_pad, a_stack, w_rows, acc):
    chans, planes_ext, rows, lanes = g_ref.shape
    in_chan, planes = a_ref.shape[:2]
    g_pad[:, 0] = jnp.zeros((planes_ext, chans, lanes), BF16)
    g_pad[:, rows + 1] = jnp.zeros((planes_ext, chans, lanes), BF16)
    for z in range(planes_ext):
        plane = g_ref[:, z].astype(F32)
        g_pad[z, 1 : rows + 1] = jnp.swapaxes(plane, 0, 1).astype(BF16)
    tail = lax.broadcasted_iota(jnp.int32, (rows, 32, lanes), 1) == 0
    for z in range(planes):
        cells = jnp.swapaxes(a_ref[:, z].astype(F32), 0, 1)
        stack = [lane_shift(cells, 1), cells, lane_shift(cells, -1), jnp.where(tail, 1.0, 0.0)]
        for part, value in enumerate(stack):
            a_stack[z * rows : (z + 1) * rows, part * 32 : part * 32 + 32] = value.astype(BF16)
    for zy in range(9):
        joined = jnp.concatenate([w_ref[3 * zy + dx].astype(F32) for dx in range(3)], axis=1)
        w_rows[:, zy * chans : (zy + 1) * chans] = joined.T.astype(BF16)
    acc[...] = jnp.zeros_like(acc)
    for z in range(planes):
        outs = []
        for y in range(0, rows, 2):
            blocks = []
            for dz in (-1, 0, 1):
                for dy in (-1, 0, 1):
                    blocks.append(
                        jnp.concatenate(
                            [g_pad[z + 1 - dz, y + 1 - dy], g_pad[z + 1 - dz, y + 2 - dy]], axis=1
                        )
                    )
            stacked = jnp.concatenate(blocks, axis=0)
            cells = jnp.concatenate([a_stack[z * rows + y], a_stack[z * rows + y + 1]], axis=1)
            acc[...] += lax.dot_general(
                stacked, cells, (((1,), (1,)), ((), ())), preferred_element_type=F32
            )
            mixed = jnp.dot(w_rows[...], stacked, preferred_element_type=F32)
            for half in range(2):
                part = mixed[:, half * lanes : (half + 1) * lanes]
                outs.append(
                    part[32:64] + lane_shift(part[0:32], -1) + lane_shift(part[64:96], 1)
                )
        gi_ref[:, z] = jnp.swapaxes(jnp.stack(outs), 0, 1).astype(BF16)
    for block in range(gw_ref.shape[0]):
        gw_ref[block] = acc[block * 4 : block * 4 + 4]


def compute(g_ext, activations, weight):
    chans, planes_ext, rows, lanes = g_ext.shape
    in_chan, planes = activations.shape[:2]
    vmem = pl.BlockSpec(memory_space=pltpu.VMEM)
    return pl.pallas_call(
        compute_kernel,
        out_shape=(
            jax.ShapeDtypeStruct(activations.shape, BF16),
            jax.ShapeDtypeStruct((144, 4, 128), F32),
        ),
        in_specs=[vmem] * 3,
        out_specs=(vmem, vmem),
        scratch_shapes=[
            pltpu.VMEM((planes_ext, rows + 2, chans, lanes), BF16),
            pltpu.VMEM((planes * rows, 128, lanes), BF16),
            pltpu.VMEM((96, 9 * chans), BF16),
            pltpu.VMEM((9 * chans, 128), F32),
        ],
        compiler_params=pltpu.CompilerParams(vmem_limit_bytes=48 << 20),
        name="products",
    )(g_ext, activations, weight)


def reduce_kernel(n, factor, x_ref, out_ref, first, second, third, send_sem, recv_sem):
    half = n // 2
    members = 2 * n
    unit = x_ref.shape[0] // (3 * members)
    slab, sample = lax.axis_index("slab"), lax.axis_index("sample")
    core = sample % 2
    place = (
        (slab // n) * half + (sample // 2) % half,
        slab % n,
        sample // n,
    )

    def device(axis, coordinate, other):
        x, y, z = (coordinate if axis == i else place[i] for i in range(3))
        return {"slab": (x // half) * n + y, "sample": z * n + (x % half) * 2 + other}

    def wide(axis, step):
        index = (place[axis] * 2 + core + step) % members
        return index, device(axis, index // 2, index % 2)

    def narrow(axis, step):
        index = (place[axis] + step) % n
        return index, device(axis, index, core)

    barrier = pltpu.get_barrier_semaphore()
    for axis in range(3):

        @pl.loop(1, members)
        def _(step, axis=axis):
            pl.semaphore_signal(
                barrier, inc=1, device_id=wide(axis, step)[1], device_id_type=MESH
            )

    pl.semaphore_wait(barrier, 3 * (members - 1))

    def copy(source, target, phase, part, peer):
        return pltpu.make_async_remote_copy(
            src_ref=source,
            dst_ref=target,
            send_sem=send_sem.at[phase, part],
            recv_sem=recv_sem.at[phase, part],
            device_id=peer,
            device_id_type=MESH,
        )

    def whole(buffer, count, sem):
        pltpu.make_async_copy(buffer.at[pl.ds(0, count)], buffer.at[pl.ds(0, count)], sem).wait()

    own = [place[part] * 2 + core for part in range(3)]
    for part in range(3):

        @pl.loop(1, members)
        def _(step, part=part):
            index, peer = wide(part, step)
            copy(
                x_ref.at[pl.ds((part * members + index) * unit, unit)],
                first.at[part, pl.ds(own[part] * unit, unit)],
                0,
                part,
                peer,
            ).start()

    for part in range(3):
        first[part, pl.ds(own[part] * unit, unit)] = x_ref[
            pl.ds((part * members + own[part]) * unit, unit)
        ]
        whole(first.at[part], (members - 1) * unit, recv_sem.at[0, part])
        total = first[part, pl.ds(0, unit)]
        for index in range(1, members):
            total = total + first[part, pl.ds(index * unit, unit)]
        axis = (part + 1) % 3
        mine = pl.ds(place[axis] * unit, unit)
        second[part, mine] = total

        @pl.loop(1, n)
        def _(step, part=part, axis=axis, mine=mine):
            copy(second.at[part, mine], second.at[part, mine], 1, part, narrow(axis, step)[1]).start()

    for part in range(3):
        whole(second.at[part], (n - 1) * unit, recv_sem.at[1, part])
        total = second[part, pl.ds(0, unit)]
        for index in range(1, n):
            total = total + second[part, pl.ds(index * unit, unit)]
        axis = (part + 2) % 3
        mine = pl.ds(place[axis] * unit, unit)
        third[part, mine] = total

        @pl.loop(1, n)
        def _(step, part=part, axis=axis, mine=mine):
            copy(third.at[part, mine], third.at[part, mine], 2, part, narrow(axis, step)[1]).start()

    for part in range(3):
        whole(third.at[part], (n - 1) * unit, recv_sem.at[2, part])
        total = third[part, pl.ds(0, unit)]
        for index in range(1, n):
            total = total + third[part, pl.ds(index * unit, unit)]
        mine = pl.ds((part * members + own[part]) * unit, unit)
        out_ref[mine] = total * factor

        @pl.loop(1, members)
        def _(step, part=part, mine=mine):
            copy(out_ref.at[mine], out_ref.at[mine], 3, part, wide(part, step)[1]).start()

    for part in range(3):
        whole(out_ref, (members - 1) * unit, recv_sem.at[3, part])
    for part in range(3):
        whole(out_ref, (members - 1) * unit, send_sem.at[0, part])
        whole(out_ref, (n - 1) * unit, send_sem.at[1, part])
        whole(out_ref, (n - 1) * unit, send_sem.at[2, part])
        whole(out_ref, (members - 1) * unit, send_sem.at[3, part])


def reduce_all(partial, n, factor):
    members = 2 * n
    unit = partial.shape[0] // (3 * members)
    vmem = pl.BlockSpec(memory_space=pltpu.VMEM)
    return pl.pallas_call(
        functools.partial(reduce_kernel, n, factor),
        out_shape=jax.ShapeDtypeStruct(partial.shape, F32),
        in_specs=[vmem],
        out_specs=vmem,
        scratch_shapes=[
            pltpu.VMEM((3, members * unit, 4, 128), F32),
            pltpu.VMEM((3, n * unit, 4, 128), F32),
            pltpu.VMEM((3, n * unit, 4, 128), F32),
            pltpu.SemaphoreType.DMA((4, 3)),
            pltpu.SemaphoreType.DMA((4, 3)),
        ],
        compiler_params=pltpu.CompilerParams(collective_id=0, has_side_effects=True),
        name="total",
    )(partial)


def local(activations, grad_out, weight):
    slabs, samples = lax.axis_size("slab"), lax.axis_size("sample")
    planes = activations.shape[2]
    regrouped = lax.all_to_all(grad_out, "slab", split_axis=2, concat_axis=1, tiled=True)
    up = [(i, i + 1) for i in range(slabs - 1)]
    down = [(i + 1, i) for i in range(slabs - 1)]
    low = lax.ppermute(regrouped[:, :, planes - 1 :], "slab", up)
    high = lax.ppermute(regrouped[:, :, :1], "slab", down)
    g_ext = jnp.concatenate([low, regrouped, high], axis=2)
    grad_in, partial = compute(g_ext[0], activations[0], weight)
    cells = samples * slabs * math.prod(activations.shape[2:])
    total = reduce_all(partial, slabs // 2, 1.0 / math.sqrt(cells))
    total = total.reshape(9, 64, 128)
    gw = total[:, :, :96].reshape(9, 64, 3, 32).transpose(0, 2, 1, 3).reshape(27, 64, 32)
    return grad_in[None], gw, total[4, :, 96]


def solution(mesh):
    placed = (P("sample", None, "slab", None, None), P("sample", "slab", None, None, None), P())
    return jax.shard_map(
        local,
        mesh=mesh,
        in_specs=placed,
        out_specs=(P("sample", None, "slab", None, None), P(), P()),
        check_vma=False,
    )
```

```python
import functools
import math

import jax
import jax.numpy as jnp
from jax import lax
from jax.experimental import pallas as pl
from jax.experimental.pallas import tpu as pltpu
from jax.sharding import PartitionSpec as P

MESH = pl.DeviceIdType.MESH
F32 = jnp.float32
BF16 = jnp.bfloat16


def lane_shift(value, shift):
    lane = lax.broadcasted_iota(jnp.int32, value.shape, value.ndim - 1)
    rolled = pltpu.roll(value, shift % 128, value.ndim - 1)
    edge = 0 if shift > 0 else 127
    return jnp.where(lane == edge, 0.0, rolled)


def far_out(middle, send):
    send(middle)

    @pl.loop(1, middle)
    def _(step):
        send(middle + step)
        send(middle - step)


def unpack_kernel(gi_hbm, final, gi_out, gw_ref, gb_ref, flat, sem):
    move = pltpu.make_async_copy(gi_hbm, gi_out, sem)
    move.start()
    for block in range(112):
        flat[block * 4 : block * 4 + 4] = final[block]
    for spot, dz in enumerate((0, 2, 1)):
        for dx in range(3):
            start = spot * 96 + dx * 32
            for dy in range(2):
                gw_ref[9 * dz + 3 * dy + dx] = flat[start : start + 32, dy * 64 : dy * 64 + 64]
            for row in (start, start + 16):
                lane, line = (row // 144) * 64, 288 + row % 144
                gw_ref[9 * dz + 6 + dx, row - start : row - start + 16] = flat[
                    line : line + 16, lane : lane + 64
                ]
    gb_ref[...] = flat[432:433, 64:128]
    move.wait()


def fused_kernel(
    n,
    factor,
    a_hbm,
    g_hbm,
    w_hbm,
    gi_hbm,
    final_hbm,
    a_own,
    a_halo,
    g_own,
    g_halo,
    w_own,
    g_pad,
    a_stack,
    w_rows,
    acc,
    flat,
    first,
    second,
    third,
    partial,
    result,
    gi_own,
    load_sem,
    keep_sem,
    swap_sem,
    halo_send,
    halo_recv,
    send_sem,
    recv_sem,
):
    in_chan, planes, rows, lanes = a_own.shape
    chans = g_own.shape[0]
    slabs = 2 * n
    share = chans // slabs
    half = n // 2
    members = 2 * n
    scale = first.shape[0] // (7 * members)
    units = (3 * scale, 2 * scale, 2 * scale)
    base = (0, 3 * scale, 5 * scale)
    slab, sample = lax.axis_index("slab"), lax.axis_index("sample")
    core = lax.rem(sample, 2)
    place = (
        lax.div(slab, n) * half + lax.rem(lax.div(sample, 2), half),
        lax.rem(slab, n),
        lax.div(sample, n),
    )
    own = [place[part] * 2 + core for part in range(3)]

    def device(axis, coordinate, other):
        x, y, z = (coordinate if axis == i else place[i] for i in range(3))
        return {
            "slab": lax.div(x, half) * n + y,
            "sample": z * n + lax.rem(x, half) * 2 + other,
        }

    def wide(axis, step):
        index = lax.rem(own[axis] + step, members)
        return index, device(axis, lax.div(index, 2), lax.rem(index, 2))

    def narrow(axis, step):
        index = lax.rem(place[axis] + step, n)
        return index, device(axis, index, core)

    load_a = pltpu.make_async_copy(a_hbm, a_own, load_sem.at[0])
    load_w = pltpu.make_async_copy(w_hbm, w_own, load_sem.at[1])
    load_g = pltpu.make_async_copy(
        g_hbm.at[:, pl.ds(slab * planes, planes)],
        g_own.at[pl.ds(slab * share, share)],
        load_sem.at[2],
    )
    load_a.start()
    load_w.start()
    load_g.start()

    barrier = pltpu.get_barrier_semaphore()

    column, side = lax.rem(slab, n), lax.div(slab, n)

    def other_slab(cross, step):
        return lax.rem(side + cross, 2) * n + lax.rem(column + step, n)

    def greet(peer):
        pl.semaphore_signal(barrier, inc=1, device_id=peer, device_id_type=MESH)

    def greet_step(step):
        greet({"slab": other_slab(1, step)})
        for axis in range(3):
            index = lax.rem(place[axis] + step, n)
            greet(device(axis, index, core))
            greet(device(axis, index, 1 - core))

    far_out(half, greet_step)

    greet(device(0, place[0], 1 - core))
    pl.semaphore_wait(barrier, 7 * (n - 1) + 1)

    def whole(buffer, count, sem):
        view = buffer.at[pl.ds(0, count)]
        pltpu.make_async_copy(view, view, sem).wait()

    def swap(cross, step):
        target = other_slab(cross, step)
        pltpu.make_async_remote_copy(
            src_ref=g_hbm.at[:, pl.ds(target * planes, planes)],
            dst_ref=g_own.at[pl.ds(slab * share, share)],
            send_sem=swap_sem.at[0],
            recv_sem=swap_sem.at[1],
            device_id={"slab": target},
            device_id_type=MESH,
        ).start()

    def halo_copy(source, target, which, side, peer):
        return pltpu.make_async_remote_copy(
            src_ref=source,
            dst_ref=target,
            send_sem=halo_send.at[which, side],
            recv_sem=halo_recv.at[which, side],
            device_id={"slab": peer},
            device_id_type=MESH,
        )

    def halo_pair(source, target, which):
        up = halo_copy(source.at[:, planes - 1], target.at[0], which, 0, lax.rem(slab + 1, slabs))
        down = halo_copy(source.at[:, 0], target.at[1], which, 1, lax.rem(slab + slabs - 1, slabs))
        return up, down

    def halo_start(pair):
        pl.when(slab < slabs - 1)(pair[0].start)
        pl.when(slab > 0)(pair[1].start)

    def halo_arrive(pair, target):
        @pl.when(slab > 0)
        def _():
            pair[0].wait_recv()

        @pl.when(slab == 0)
        def _():
            target[0] = jnp.zeros(target.shape[1:], target.dtype)

        @pl.when(slab < slabs - 1)
        def _():
            pair[1].wait_recv()

        @pl.when(slab == slabs - 1)
        def _():
            target[1] = jnp.zeros(target.shape[1:], target.dtype)

    def halo_sent(pair):
        pl.when(slab < slabs - 1)(pair[0].wait_send)
        pl.when(slab > 0)(pair[1].wait_send)

    load_a.wait()
    a_pair = halo_pair(a_own, a_halo, 0)
    halo_start(a_pair)

    far_first = sorted(range(n), key=lambda step: -min(step, n - step))
    for step in far_first:
        swap(1, step)
        if step:
            swap(0, step)

    for z in range(planes + 2):
        g_pad[z, 0] = jnp.zeros((chans, lanes), BF16)
        g_pad[z, rows + 1] = jnp.zeros((chans, lanes), BF16)

    tail = lax.broadcasted_iota(jnp.int32, (rows, 32, lanes), 1) == 0

    def stack_plane(z, plane):
        cells = jnp.swapaxes(plane.astype(F32), 0, 1)
        stack = [lane_shift(cells, 1), cells, lane_shift(cells, -1), jnp.where(tail, 1.0, 0.0)]
        for part, value in enumerate(stack):
            a_stack[z, :, part * 32 : part * 32 + 32] = value.astype(BF16)

    def pad_plane(z, plane):
        g_pad[z, 1 : rows + 1] = jnp.swapaxes(plane.astype(F32), 0, 1).astype(BF16)

    for z in range(planes):
        stack_plane(z + 1, a_own[:, z])
    load_w.wait()
    for zy in range(9):
        for dx in range(3):
            w_rows[dx * 32 : dx * 32 + 32, zy * chans : (zy + 1) * chans] = w_own[3 * zy + dx]
    halo_arrive(a_pair, a_halo)
    stack_plane(0, a_halo[0])
    stack_plane(planes + 1, a_halo[1])

    load_g.wait()
    whole(g_own, chans - share, swap_sem.at[1])
    g_pair = halo_pair(g_own, g_halo, 1)
    halo_start(g_pair)
    for z in range(planes):
        pad_plane(z + 1, g_own[:, z])

    total = None
    for z in range(planes):
        cot = jnp.concatenate(
            [
                jnp.concatenate([g_pad[z + 1, y + 1 - dy] for y in range(rows)], axis=1)
                for dy in (-1, 0, 1)
            ],
            axis=0,
        )
        cells = jnp.concatenate(
            [
                jnp.concatenate([a_stack[z + 1 + dz, y, :height] for y in range(rows)], axis=1)
                for dz, height in ((-1, 96), (1, 96), (0, 112))
            ],
            axis=0,
        )
        term = lax.dot_general(
            cells, cot, (((1,), (1,)), ((), ())), preferred_element_type=F32
        )
        if z == 0:
            acc[:, 0:192] = term
        else:
            acc[:, 0:192] += term
    low = lax.broadcasted_iota(jnp.int32, (144, 128), 1) < 64
    flat[0:144] = jnp.where(low, acc[0:144, 128:256], pltpu.roll(acc[144:288, 128:256], 64, 1))
    for block in range(112):
        if block < 72:
            partial[block] = acc[block * 4 : block * 4 + 4, 0:128]
        elif block < 108:
            partial[block] = flat[block * 4 - 288 : block * 4 - 284]
        else:
            partial[block] = acc[block * 4 - 144 : block * 4 - 140, 0:128]

    def copy(source, target, phase, part, peer):
        return pltpu.make_async_remote_copy(
            src_ref=source,
            dst_ref=target,
            send_sem=send_sem.at[phase, part],
            recv_sem=recv_sem.at[phase, part],
            device_id=peer,
            device_id_type=MESH,
        )

    def piece(part, index, count=members):
        return pl.ds(base[part] * count + index * units[part], units[part])

    def scatter(step):
        for part in range(3):
            index, peer = wide(part, step)
            copy(
                partial.at[piece(part, index)], first.at[piece(part, own[part])], 0, part, peer
            ).start()

    far_out(n, scatter)

    def inputs_plane(z):
        outs = []
        for y in range(0, rows, 2):
            stacked = jnp.concatenate(
                [
                    jnp.concatenate(
                        [g_pad[z + 1 - dz, y + 1 - dy], g_pad[z + 1 - dz, y + 2 - dy]], axis=1
                    )
                    for dz in (-1, 0, 1)
                    for dy in (-1, 0, 1)
                ],
                axis=0,
            )
            mixed = jnp.dot(w_rows[...], stacked, preferred_element_type=F32)
            for side in range(2):
                part = mixed[:, side * lanes : (side + 1) * lanes]
                outs.append(
                    part[32:64] + lane_shift(part[0:32], -1) + lane_shift(part[64:96], 1)
                )
        gi_own[:, z] = jnp.swapaxes(jnp.stack(outs), 0, 1).astype(BF16)

    for z in range(1, planes - 1):
        inputs_plane(z)

    def add_up(buffer, part, count):
        total = buffer[piece(part, 0, count)]
        for index in range(1, count):
            total = total + buffer[piece(part, index, count)]
        return total

    for part in range(3):
        first[piece(part, own[part])] = partial[piece(part, own[part])]
        whole(first, (members - 1) * units[part], recv_sem.at[0, part])
        axis = (part + 1) % 3
        mine = piece(part, place[axis], n)
        second[mine] = add_up(first, part, members)

        def spread(step, part=part, axis=axis, mine=mine):
            copy(second.at[mine], second.at[mine], 1, part, narrow(axis, step)[1]).start()

        far_out(half, spread)

    halo_arrive(g_pair, g_halo)
    pad_plane(0, g_halo[0])
    pad_plane(planes + 1, g_halo[1])
    inputs_plane(0)
    inputs_plane(planes - 1)
    save_gi = pltpu.make_async_copy(gi_own, gi_hbm, keep_sem.at[3])
    save_gi.start()

    for part in range(3):
        whole(second, (n - 1) * units[part], recv_sem.at[1, part])
        axis = (part + 2) % 3
        mine = piece(part, place[axis], n)
        third[mine] = add_up(second, part, n)

        def spread(step, part=part, axis=axis, mine=mine):
            copy(third.at[mine], third.at[mine], 2, part, narrow(axis, step)[1]).start()

        far_out(half, spread)

    for part in range(3):
        whole(first, (members - 1) * units[part], send_sem.at[0, part])

    keep_own = [
        pltpu.make_async_copy(
            result.at[piece(part, own[part])],
            final_hbm.at[piece(part, own[part])],
            keep_sem.at[part],
        )
        for part in range(3)
    ]

    for part in range(3):
        whole(third, (n - 1) * units[part], recv_sem.at[2, part])
        mine = piece(part, own[part])
        result[mine] = add_up(third, part, n) * factor
        keep_own[part].start()

        def spread(step, part=part, mine=mine):
            copy(result.at[mine], final_hbm.at[mine], 3, part, wide(part, step)[1]).start()

        far_out(n, spread)

    for part in range(3):
        whole(final_hbm, (members - 1) * units[part], recv_sem.at[3, part])

    for part in range(3):
        keep_own[part].wait()
    save_gi.wait()
    whole(g_own, chans - share, swap_sem.at[0])
    halo_sent(a_pair)
    halo_sent(g_pair)
    for part in range(3):
        whole(second, (n - 1) * units[part], send_sem.at[1, part])
        whole(third, (n - 1) * units[part], send_sem.at[2, part])
        whole(first, (members - 1) * units[part], send_sem.at[3, part])


def local(activations, grad_out, weight):
    slabs, samples = lax.axis_size("slab"), lax.axis_size("sample")
    n = slabs // 2
    _, in_chan, planes, rows, lanes = activations.shape
    chans = weight.shape[1]
    cells = samples * slabs * planes * rows * lanes
    vmem = pl.BlockSpec(memory_space=pltpu.VMEM)
    hbm = pl.BlockSpec(memory_space=pltpu.HBM)
    weight = weight.transpose(0, 2, 1)
    grad_in, packed = pl.pallas_call(
        functools.partial(fused_kernel, n, 1.0 / math.sqrt(cells)),
        out_shape=(
            jax.ShapeDtypeStruct(activations.shape[1:], BF16),
            jax.ShapeDtypeStruct((112, 4, 128), F32),
        ),
        in_specs=[hbm] * 3,
        out_specs=(hbm, hbm),
        scratch_shapes=[
            pltpu.VMEM((in_chan, planes, rows, lanes), BF16),
            pltpu.VMEM((2, in_chan, rows, lanes), BF16),
            pltpu.VMEM((chans, planes, rows, lanes), BF16),
            pltpu.VMEM((2, chans, rows, lanes), BF16),
            pltpu.VMEM(weight.shape, BF16),
            pltpu.VMEM((planes + 2, rows + 2, chans, lanes), BF16),
            pltpu.VMEM((planes + 2, rows, 128, lanes), BF16),
            pltpu.VMEM((96, 9 * chans), BF16),
            pltpu.VMEM((304, 256), F32),
            pltpu.VMEM((448, 128), F32),
            pltpu.VMEM((112, 4, 128), F32),
            pltpu.VMEM((56, 4, 128), F32),
            pltpu.VMEM((56, 4, 128), F32),
            pltpu.VMEM((112, 4, 128), F32),
            pltpu.VMEM((112, 4, 128), F32),
            pltpu.VMEM(activations.shape[1:], BF16),
            pltpu.SemaphoreType.DMA((3,)),
            pltpu.SemaphoreType.DMA((4,)),
            pltpu.SemaphoreType.DMA((2,)),
            pltpu.SemaphoreType.DMA((2, 2)),
            pltpu.SemaphoreType.DMA((2, 2)),
            pltpu.SemaphoreType.DMA((4, 3)),
            pltpu.SemaphoreType.DMA((4, 3)),
        ],
        compiler_params=pltpu.CompilerParams(
            collective_id=0, has_side_effects=True, vmem_limit_bytes=58 << 20
        ),
        name="backward",
    )(activations[0], grad_out[0], weight)
    grad_in, gw, gb = pl.pallas_call(
        unpack_kernel,
        out_shape=(
            jax.ShapeDtypeStruct(activations.shape[1:], BF16),
            jax.ShapeDtypeStruct(weight.shape, F32),
            jax.ShapeDtypeStruct((1, chans), F32),
        ),
        in_specs=[hbm, vmem],
        out_specs=(hbm, vmem, vmem),
        scratch_shapes=[pltpu.VMEM((448, 128), F32), pltpu.SemaphoreType.DMA],
        name="unpack",
    )(grad_in, packed)
    return grad_in[None], gw.transpose(0, 2, 1), gb[0]


def solution(mesh):
    placed = (P("sample", None, "slab", None, None), P("sample", "slab", None, None, None), P())
    return jax.shard_map(
        local,
        mesh=mesh,
        in_specs=placed,
        out_specs=(P("sample", None, "slab", None, None), P(), P()),
        check_vma=False,
    )
```

```python
import functools
import math

import jax
import jax.numpy as jnp
from jax import lax
from jax.experimental import pallas as pl
from jax.experimental.pallas import tpu as pltpu
from jax.sharding import PartitionSpec as P

MESH = pl.DeviceIdType.MESH
F32 = jnp.float32
BF16 = jnp.bfloat16


def lane_shift(value, shift):
    lane = lax.broadcasted_iota(jnp.int32, value.shape, value.ndim - 1)
    rolled = pltpu.roll(value, shift % 128, value.ndim - 1)
    edge = 0 if shift > 0 else 127
    return jnp.where(lane == edge, 0.0, rolled)


def far_out(middle, send):
    send(middle)

    @pl.loop(1, middle)
    def _(step):
        send(middle + step)
        send(middle - step)


def unpack_kernel(gi_hbm, final, gi_out, gw_ref, gb_ref, flat):
    gi_out[...] = gi_hbm[...]
    for block in range(112):
        flat[block * 4 : block * 4 + 4] = final[block]
    for spot, dz in enumerate((0, 2, 1)):
        for dx in range(3):
            start = spot * 96 + dx * 32
            for dy in range(2):
                gw_ref[9 * dz + 3 * dy + dx] = flat[start : start + 32, dy * 64 : dy * 64 + 64]
            for row in (start, start + 16):
                lane, line = (row // 144) * 64, 288 + row % 144
                gw_ref[9 * dz + 6 + dx, row - start : row - start + 16] = flat[
                    line : line + 16, lane : lane + 64
                ]
    gb_ref[...] = flat[432:433, 64:128]


def fused_kernel(
    n,
    factor,
    a_hbm,
    g_hbm,
    w_hbm,
    gi_hbm,
    final_hbm,
    a_own,
    a_halo,
    g_own,
    g_halo,
    w_own,
    g_pad,
    a_stack,
    w_rows,
    acc,
    flat,
    first,
    second,
    third,
    partial,
    result,
    gi_own,
    load_sem,
    keep_sem,
    swap_sem,
    halo_send,
    halo_recv,
    send_sem,
    recv_sem,
):
    in_chan, planes, rows, lanes = a_own.shape
    chans = g_own.shape[0]
    slabs = 2 * n
    share = chans // slabs
    half = n // 2
    members = 2 * n
    scale = first.shape[0] // (7 * members)
    units = (3 * scale, 2 * scale, 2 * scale)
    base = (0, 3 * scale, 5 * scale)
    slab, sample = lax.axis_index("slab"), lax.axis_index("sample")
    core = lax.rem(sample, 2)
    place = (
        lax.div(slab, n) * half + lax.rem(lax.div(sample, 2), half),
        lax.rem(slab, n),
        lax.div(sample, n),
    )
    own = [place[part] * 2 + core for part in range(3)]

    def device(axis, coordinate, other):
        x, y, z = (coordinate if axis == i else place[i] for i in range(3))
        return {
            "slab": lax.div(x, half) * n + y,
            "sample": z * n + lax.rem(x, half) * 2 + other,
        }

    def wide(axis, step):
        index = lax.rem(own[axis] + step, members)
        return index, device(axis, lax.div(index, 2), lax.rem(index, 2))

    def narrow(axis, step):
        index = lax.rem(place[axis] + step, n)
        return index, device(axis, index, core)

    load_a = pltpu.make_async_copy(a_hbm, a_own, load_sem.at[0])
    load_w = pltpu.make_async_copy(w_hbm, w_own, load_sem.at[1])
    load_g = pltpu.make_async_copy(
        g_hbm.at[:, pl.ds(slab * planes, planes)],
        g_own.at[pl.ds(slab * share, share)],
        load_sem.at[2],
    )
    load_a.start()
    load_w.start()
    load_g.start()

    barrier = pltpu.get_barrier_semaphore()

    column, side = lax.rem(slab, n), lax.div(slab, n)

    def other_slab(cross, step):
        return lax.rem(side + cross, 2) * n + lax.rem(column + step, n)

    def greet(peer):
        pl.semaphore_signal(barrier, inc=1, device_id=peer, device_id_type=MESH)

    def greet_step(step):
        greet({"slab": other_slab(1, step)})
        for axis in range(3):
            index = lax.rem(place[axis] + step, n)
            greet(device(axis, index, core))
            greet(device(axis, index, 1 - core))

    far_out(half, greet_step)

    greet(device(0, place[0], 1 - core))
    pl.semaphore_wait(barrier, 7 * (n - 1) + 1)

    def whole(buffer, count, sem):
        view = buffer.at[pl.ds(0, count)]
        pltpu.make_async_copy(view, view, sem).wait()

    def swap(cross, step):
        target = other_slab(cross, step)
        pltpu.make_async_remote_copy(
            src_ref=g_hbm.at[:, pl.ds(target * planes, planes)],
            dst_ref=g_own.at[pl.ds(slab * share, share)],
            send_sem=swap_sem.at[0],
            recv_sem=swap_sem.at[1],
            device_id={"slab": target},
            device_id_type=MESH,
        ).start()

    def halo_copy(source, target, which, side, peer):
        return pltpu.make_async_remote_copy(
            src_ref=source,
            dst_ref=target,
            send_sem=halo_send.at[which, side],
            recv_sem=halo_recv.at[which, side],
            device_id={"slab": peer},
            device_id_type=MESH,
        )

    def halo_pair(source, target, which):
        up = halo_copy(source.at[:, planes - 1], target.at[0], which, 0, lax.rem(slab + 1, slabs))
        down = halo_copy(source.at[:, 0], target.at[1], which, 1, lax.rem(slab + slabs - 1, slabs))
        return up, down

    def halo_start(pair):
        pl.when(slab < slabs - 1)(pair[0].start)
        pl.when(slab > 0)(pair[1].start)

    def halo_arrive(pair, target):
        @pl.when(slab > 0)
        def _():
            pair[0].wait_recv()

        @pl.when(slab == 0)
        def _():
            target[0] = jnp.zeros(target.shape[1:], target.dtype)

        @pl.when(slab < slabs - 1)
        def _():
            pair[1].wait_recv()

        @pl.when(slab == slabs - 1)
        def _():
            target[1] = jnp.zeros(target.shape[1:], target.dtype)

    def halo_sent(pair):
        pl.when(slab < slabs - 1)(pair[0].wait_send)
        pl.when(slab > 0)(pair[1].wait_send)

    load_a.wait()
    a_pair = halo_pair(a_own, a_halo, 0)
    halo_start(a_pair)

    far_first = sorted(range(n), key=lambda step: -min(step, n - step))
    for step in far_first:
        swap(1, step)
        if step:
            swap(0, step)

    for z in range(planes + 2):
        g_pad[z, 0] = jnp.zeros((chans, lanes), BF16)
        g_pad[z, rows + 1] = jnp.zeros((chans, lanes), BF16)

    tail = lax.broadcasted_iota(jnp.int32, (rows, 32, lanes), 1) == 0

    def stack_plane(z, plane):
        cells = jnp.swapaxes(plane.astype(F32), 0, 1)
        stack = [lane_shift(cells, 1), cells, lane_shift(cells, -1), jnp.where(tail, 1.0, 0.0)]
        for part, value in enumerate(stack):
            a_stack[z, :, part * 32 : part * 32 + 32] = value.astype(BF16)

    def pad_plane(z, plane):
        g_pad[z, 1 : rows + 1] = jnp.swapaxes(plane.astype(F32), 0, 1).astype(BF16)

    for z in range(planes):
        stack_plane(z + 1, a_own[:, z])
    load_w.wait()
    for zy in range(9):
        for dx in range(3):
            w_rows[dx * 32 : dx * 32 + 32, zy * chans : (zy + 1) * chans] = w_own[3 * zy + dx]
    halo_arrive(a_pair, a_halo)
    stack_plane(0, a_halo[0])
    stack_plane(planes + 1, a_halo[1])

    load_g.wait()
    whole(g_own, chans - share, swap_sem.at[1])
    g_pair = halo_pair(g_own, g_halo, 1)
    halo_start(g_pair)
    for z in range(planes):
        pad_plane(z + 1, g_own[:, z])

    total = None
    for z in range(planes):
        cot = jnp.concatenate(
            [
                jnp.concatenate([g_pad[z + 1, y + 1 - dy] for y in range(rows)], axis=1)
                for dy in (-1, 0, 1)
            ],
            axis=0,
        )
        cells = jnp.concatenate(
            [
                jnp.concatenate([a_stack[z + 1 + dz, y, :height] for y in range(rows)], axis=1)
                for dz, height in ((-1, 96), (1, 96), (0, 112))
            ],
            axis=0,
        )
        term = lax.dot_general(
            cells, cot, (((1,), (1,)), ((), ())), preferred_element_type=F32
        )
        if z == 0:
            acc[:, 0:192] = term
        else:
            acc[:, 0:192] += term
    low = lax.broadcasted_iota(jnp.int32, (144, 128), 1) < 64
    flat[0:144] = jnp.where(low, acc[0:144, 128:256], pltpu.roll(acc[144:288, 128:256], 64, 1))
    for block in range(112):
        if block < 72:
            partial[block] = acc[block * 4 : block * 4 + 4, 0:128]
        elif block < 108:
            partial[block] = flat[block * 4 - 288 : block * 4 - 284]
        else:
            partial[block] = acc[block * 4 - 144 : block * 4 - 140, 0:128]

    def copy(source, target, phase, part, peer):
        return pltpu.make_async_remote_copy(
            src_ref=source,
            dst_ref=target,
            send_sem=send_sem.at[phase, part],
            recv_sem=recv_sem.at[phase, part],
            device_id=peer,
            device_id_type=MESH,
        )

    def piece(part, index, count=members):
        return pl.ds(base[part] * count + index * units[part], units[part])

    def scatter(step):
        for part in range(3):
            index, peer = wide(part, step)
            copy(
                partial.at[piece(part, index)], first.at[piece(part, own[part])], 0, part, peer
            ).start()

    far_out(n, scatter)

    def inputs_plane(z):
        outs = []
        for y in range(0, rows, 2):
            stacked = jnp.concatenate(
                [
                    jnp.concatenate(
                        [g_pad[z + 1 - dz, y + 1 - dy], g_pad[z + 1 - dz, y + 2 - dy]], axis=1
                    )
                    for dz in (-1, 0, 1)
                    for dy in (-1, 0, 1)
                ],
                axis=0,
            )
            mixed = jnp.dot(w_rows[...], stacked, preferred_element_type=F32)
            for side in range(2):
                part = mixed[:, side * lanes : (side + 1) * lanes]
                outs.append(
                    part[32:64] + lane_shift(part[0:32], -1) + lane_shift(part[64:96], 1)
                )
        gi_own[:, z] = jnp.swapaxes(jnp.stack(outs), 0, 1).astype(BF16)

    for z in range(1, planes - 1):
        inputs_plane(z)

    def add_up(buffer, part, count):
        total = buffer[piece(part, 0, count)]
        for index in range(1, count):
            total = total + buffer[piece(part, index, count)]
        return total

    for part in range(3):
        first[piece(part, own[part])] = partial[piece(part, own[part])]
        whole(first, (members - 1) * units[part], recv_sem.at[0, part])
        axis = (part + 1) % 3
        mine = piece(part, place[axis], n)
        second[mine] = add_up(first, part, members)

        def spread(step, part=part, axis=axis, mine=mine):
            copy(second.at[mine], second.at[mine], 1, part, narrow(axis, step)[1]).start()

        far_out(half, spread)

    halo_arrive(g_pair, g_halo)
    pad_plane(0, g_halo[0])
    pad_plane(planes + 1, g_halo[1])
    inputs_plane(0)
    inputs_plane(planes - 1)
    save_gi = pltpu.make_async_copy(gi_own, gi_hbm, keep_sem.at[3])
    save_gi.start()

    for part in range(3):
        whole(second, (n - 1) * units[part], recv_sem.at[1, part])
        axis = (part + 2) % 3
        mine = piece(part, place[axis], n)
        third[mine] = add_up(second, part, n)

        def spread(step, part=part, axis=axis, mine=mine):
            copy(third.at[mine], third.at[mine], 2, part, narrow(axis, step)[1]).start()

        far_out(half, spread)

    for part in range(3):
        whole(first, (members - 1) * units[part], send_sem.at[0, part])

    keep_own = [
        pltpu.make_async_copy(
            result.at[piece(part, own[part])],
            final_hbm.at[piece(part, own[part])],
            keep_sem.at[part],
        )
        for part in range(3)
    ]

    for part in range(3):
        whole(third, (n - 1) * units[part], recv_sem.at[2, part])
        mine = piece(part, own[part])
        result[mine] = add_up(third, part, n) * factor
        keep_own[part].start()

        def spread(step, part=part, mine=mine):
            copy(result.at[mine], final_hbm.at[mine], 3, part, wide(part, step)[1]).start()

        far_out(n, spread)

    for part in range(3):
        whole(final_hbm, (members - 1) * units[part], recv_sem.at[3, part])

    for part in range(3):
        keep_own[part].wait()
    save_gi.wait()
    whole(g_own, chans - share, swap_sem.at[0])
    halo_sent(a_pair)
    halo_sent(g_pair)
    for part in range(3):
        whole(second, (n - 1) * units[part], send_sem.at[1, part])
        whole(third, (n - 1) * units[part], send_sem.at[2, part])
        whole(first, (members - 1) * units[part], send_sem.at[3, part])


def local(activations, grad_out, weight):
    slabs, samples = lax.axis_size("slab"), lax.axis_size("sample")
    n = slabs // 2
    _, in_chan, planes, rows, lanes = activations.shape
    chans = weight.shape[1]
    cells = samples * slabs * planes * rows * lanes
    vmem = pl.BlockSpec(memory_space=pltpu.VMEM)
    hbm = pl.BlockSpec(memory_space=pltpu.HBM)
    weight = weight.transpose(0, 2, 1)
    grad_in, packed = pl.pallas_call(
        functools.partial(fused_kernel, n, 1.0 / math.sqrt(cells)),
        out_shape=(
            jax.ShapeDtypeStruct(activations.shape[1:], BF16),
            jax.ShapeDtypeStruct((112, 4, 128), F32),
        ),
        in_specs=[hbm] * 3,
        out_specs=(hbm, hbm),
        scratch_shapes=[
            pltpu.VMEM((in_chan, planes, rows, lanes), BF16),
            pltpu.VMEM((2, in_chan, rows, lanes), BF16),
            pltpu.VMEM((chans, planes, rows, lanes), BF16),
            pltpu.VMEM((2, chans, rows, lanes), BF16),
            pltpu.VMEM(weight.shape, BF16),
            pltpu.VMEM((planes + 2, rows + 2, chans, lanes), BF16),
            pltpu.VMEM((planes + 2, rows, 128, lanes), BF16),
            pltpu.VMEM((96, 9 * chans), BF16),
            pltpu.VMEM((304, 256), F32),
            pltpu.VMEM((448, 128), F32),
            pltpu.VMEM((112, 4, 128), F32),
            pltpu.VMEM((56, 4, 128), F32),
            pltpu.VMEM((56, 4, 128), F32),
            pltpu.VMEM((112, 4, 128), F32),
            pltpu.VMEM((112, 4, 128), F32),
            pltpu.VMEM(activations.shape[1:], BF16),
            pltpu.SemaphoreType.DMA((3,)),
            pltpu.SemaphoreType.DMA((4,)),
            pltpu.SemaphoreType.DMA((2,)),
            pltpu.SemaphoreType.DMA((2, 2)),
            pltpu.SemaphoreType.DMA((2, 2)),
            pltpu.SemaphoreType.DMA((4, 3)),
            pltpu.SemaphoreType.DMA((4, 3)),
        ],
        compiler_params=pltpu.CompilerParams(
            collective_id=0, has_side_effects=True, vmem_limit_bytes=58 << 20
        ),
        name="backward",
    )(activations[0], grad_out[0], weight)
    grad_in, gw, gb = pl.pallas_call(
        unpack_kernel,
        out_shape=(
            jax.ShapeDtypeStruct(activations.shape[1:], BF16),
            jax.ShapeDtypeStruct(weight.shape, F32),
            jax.ShapeDtypeStruct((1, chans), F32),
        ),
        in_specs=[vmem, vmem],
        out_specs=(vmem, vmem, vmem),
        scratch_shapes=[pltpu.VMEM((448, 128), F32)],
        name="unpack",
    )(grad_in, packed)
    return grad_in[None], gw.transpose(0, 2, 1), gb[0]


def solution(mesh):
    placed = (P("sample", None, "slab", None, None), P("sample", "slab", None, None, None), P())
    return jax.shard_map(
        local,
        mesh=mesh,
        in_specs=placed,
        out_specs=(P("sample", None, "slab", None, None), P(), P()),
        check_vma=False,
    )
```

```python
import functools
import math

import jax
import jax.numpy as jnp
from jax import lax
from jax.experimental import pallas as pl
from jax.experimental.pallas import tpu as pltpu
from jax.sharding import PartitionSpec as P

MESH = pl.DeviceIdType.MESH
F32 = jnp.float32
BF16 = jnp.bfloat16


def lane_shift(value, shift):
    lane = lax.broadcasted_iota(jnp.int32, value.shape, value.ndim - 1)
    rolled = pltpu.roll(value, shift % 128, value.ndim - 1)
    edge = 0 if shift > 0 else 127
    return jnp.where(lane == edge, 0.0, rolled)


def far_out(middle, send):
    send(middle)

    @pl.loop(1, middle)
    def _(step):
        send(middle + step)
        send(middle - step)


def unpack_kernel(gi_hbm, final, gi_out, gw_ref, gb_ref, flat):
    gi_out[...] = gi_hbm[...]
    for block in range(112):
        flat[block * 4 : block * 4 + 4] = final[block]
    for spot, dz in enumerate((0, 2, 1)):
        for dx in range(3):
            start = spot * 96 + dx * 32
            for dy in range(2):
                gw_ref[9 * dz + 3 * dy + dx] = flat[start : start + 32, dy * 64 : dy * 64 + 64]
            for row in (start, start + 16):
                lane, line = (row // 144) * 64, 288 + row % 144
                gw_ref[9 * dz + 6 + dx, row - start : row - start + 16] = flat[
                    line : line + 16, lane : lane + 64
                ]
    gb_ref[...] = flat[432:433, 64:128]


def fused_kernel(
    n,
    factor,
    a_hbm,
    g_hbm,
    w_hbm,
    gi_hbm,
    final_hbm,
    a_own,
    a_halo,
    g_own,
    g_halo,
    w_own,
    g_pad,
    a_stack,
    w_rows,
    acc,
    flat,
    first,
    second,
    third,
    partial,
    result,
    gi_own,
    load_sem,
    keep_sem,
    swap_sem,
    halo_send,
    halo_recv,
    send_sem,
    recv_sem,
):
    in_chan, planes, rows, lanes = a_own.shape
    chans = g_own.shape[0]
    slabs = 2 * n
    share = chans // slabs
    half = n // 2
    members = 2 * n
    scale = first.shape[0] // (7 * members)
    units = (3 * scale, 2 * scale, 2 * scale)
    base = (0, 3 * scale, 5 * scale)
    slab, sample = lax.axis_index("slab"), lax.axis_index("sample")
    core = lax.rem(sample, 2)
    place = (
        lax.div(slab, n) * half + lax.rem(lax.div(sample, 2), half),
        lax.rem(slab, n),
        lax.div(sample, n),
    )
    own = [place[part] * 2 + core for part in range(3)]

    def device(axis, coordinate, other):
        x, y, z = (coordinate if axis == i else place[i] for i in range(3))
        return {
            "slab": lax.div(x, half) * n + y,
            "sample": z * n + lax.rem(x, half) * 2 + other,
        }

    def wide(axis, step):
        index = lax.rem(own[axis] + step, members)
        return index, device(axis, lax.div(index, 2), lax.rem(index, 2))

    def narrow(axis, step):
        index = lax.rem(place[axis] + step, n)
        return index, device(axis, index, core)

    load_a = pltpu.make_async_copy(a_hbm, a_own, load_sem.at[0])
    load_w = pltpu.make_async_copy(w_hbm, w_own, load_sem.at[1])
    load_g = pltpu.make_async_copy(
        g_hbm.at[:, pl.ds(slab * planes, planes)],
        g_own.at[pl.ds(slab * share, share)],
        load_sem.at[2],
    )
    load_a.start()
    load_w.start()
    load_g.start()

    barrier = pltpu.get_barrier_semaphore()

    column, side = lax.rem(slab, n), lax.div(slab, n)

    def other_slab(cross, step):
        return lax.rem(side + cross, 2) * n + lax.rem(column + step, n)

    def greet(peer):
        pl.semaphore_signal(barrier, inc=1, device_id=peer, device_id_type=MESH)

    def greet_step(step):
        greet({"slab": other_slab(1, step)})
        for axis in range(3):
            index = lax.rem(place[axis] + step, n)
            greet(device(axis, index, core))
            greet(device(axis, index, 1 - core))

    far_out(half, greet_step)

    greet(device(0, place[0], 1 - core))
    pl.semaphore_wait(barrier, 7 * (n - 1) + 1)

    def whole(buffer, count, sem):
        view = buffer.at[pl.ds(0, count)]
        pltpu.make_async_copy(view, view, sem).wait()

    def swap(cross, step):
        target = other_slab(cross, step)
        pltpu.make_async_remote_copy(
            src_ref=g_hbm.at[:, pl.ds(target * planes, planes)],
            dst_ref=g_own.at[pl.ds(slab * share, share)],
            send_sem=swap_sem.at[0],
            recv_sem=swap_sem.at[1],
            device_id={"slab": target},
            device_id_type=MESH,
        ).start()

    def halo_copy(source, target, which, side, peer):
        return pltpu.make_async_remote_copy(
            src_ref=source,
            dst_ref=target,
            send_sem=halo_send.at[which, side],
            recv_sem=halo_recv.at[which, side],
            device_id={"slab": peer},
            device_id_type=MESH,
        )

    def halo_pair(source, target, which):
        up = halo_copy(source.at[:, planes - 1], target.at[0], which, 0, lax.rem(slab + 1, slabs))
        down = halo_copy(source.at[:, 0], target.at[1], which, 1, lax.rem(slab + slabs - 1, slabs))
        return up, down

    def halo_start(pair):
        pl.when(slab < slabs - 1)(pair[0].start)
        pl.when(slab > 0)(pair[1].start)

    def halo_arrive(pair, target):
        @pl.when(slab > 0)
        def _():
            pair[0].wait_recv()

        @pl.when(slab == 0)
        def _():
            target[0] = jnp.zeros(target.shape[1:], target.dtype)

        @pl.when(slab < slabs - 1)
        def _():
            pair[1].wait_recv()

        @pl.when(slab == slabs - 1)
        def _():
            target[1] = jnp.zeros(target.shape[1:], target.dtype)

    def halo_sent(pair):
        pl.when(slab < slabs - 1)(pair[0].wait_send)
        pl.when(slab > 0)(pair[1].wait_send)

    load_a.wait()
    a_pair = halo_pair(a_own, a_halo, 0)
    halo_start(a_pair)

    far_first = sorted(range(n), key=lambda step: -min(step, n - step))
    for step in far_first:
        swap(1, step)
        if step:
            swap(0, step)

    for z in range(planes + 2):
        g_pad[z, 0] = jnp.zeros((chans, lanes), BF16)
        g_pad[z, rows + 1] = jnp.zeros((chans, lanes), BF16)

    tail = lax.broadcasted_iota(jnp.int32, (rows, 32, lanes), 1) == 0

    def stack_plane(z, plane):
        cells = jnp.swapaxes(plane.astype(F32), 0, 1)
        stack = [lane_shift(cells, 1), cells, lane_shift(cells, -1), jnp.where(tail, 1.0, 0.0)]
        for part, value in enumerate(stack):
            a_stack[z, :, part * 32 : part * 32 + 32] = value.astype(BF16)

    def pad_plane(z, plane):
        g_pad[z, 1 : rows + 1] = jnp.swapaxes(plane.astype(F32), 0, 1).astype(BF16)

    for z in range(planes):
        stack_plane(z + 1, a_own[:, z])
    load_w.wait()
    for zy in range(9):
        for dx in range(3):
            w_rows[dx * 32 : dx * 32 + 32, zy * chans : (zy + 1) * chans] = w_own[3 * zy + dx]
    halo_arrive(a_pair, a_halo)
    stack_plane(0, a_halo[0])
    stack_plane(planes + 1, a_halo[1])

    load_g.wait()
    whole(g_own, chans - share, swap_sem.at[1])
    g_pair = halo_pair(g_own, g_halo, 1)
    for z in range(planes):
        pad_plane(z + 1, g_own[:, z])

    total = None
    for z in range(planes):
        cot = jnp.concatenate(
            [
                jnp.concatenate([g_pad[z + 1, y + 1 - dy] for y in range(rows)], axis=1)
                for dy in (-1, 0, 1)
            ],
            axis=0,
        )
        cells = jnp.concatenate(
            [
                jnp.concatenate([a_stack[z + 1 + dz, y, :height] for y in range(rows)], axis=1)
                for dz, height in ((-1, 96), (1, 96), (0, 112))
            ],
            axis=0,
        )
        term = lax.dot_general(
            cells, cot, (((1,), (1,)), ((), ())), preferred_element_type=F32
        )
        if z == 0:
            acc[:, 0:192] = term
        else:
            acc[:, 0:192] += term
    low = lax.broadcasted_iota(jnp.int32, (144, 128), 1) < 64
    flat[0:144] = jnp.where(low, acc[0:144, 128:256], pltpu.roll(acc[144:288, 128:256], 64, 1))
    for block in range(112):
        if block < 72:
            partial[block] = acc[block * 4 : block * 4 + 4, 0:128]
        elif block < 108:
            partial[block] = flat[block * 4 - 288 : block * 4 - 284]
        else:
            partial[block] = acc[block * 4 - 144 : block * 4 - 140, 0:128]

    def copy(source, target, phase, part, peer):
        return pltpu.make_async_remote_copy(
            src_ref=source,
            dst_ref=target,
            send_sem=send_sem.at[phase, part],
            recv_sem=recv_sem.at[phase, part],
            device_id=peer,
            device_id_type=MESH,
        )

    def piece(part, index, count=members):
        return pl.ds(base[part] * count + index * units[part], units[part])

    def scatter(step):
        for part in range(3):
            index, peer = wide(part, step)
            copy(
                partial.at[piece(part, index)], first.at[piece(part, own[part])], 0, part, peer
            ).start()

    far_out(n, scatter)
    halo_start(g_pair)

    def inputs_plane(z):
        outs = []
        for y in range(0, rows, 2):
            stacked = jnp.concatenate(
                [
                    jnp.concatenate(
                        [g_pad[z + 1 - dz, y + 1 - dy], g_pad[z + 1 - dz, y + 2 - dy]], axis=1
                    )
                    for dz in (-1, 0, 1)
                    for dy in (-1, 0, 1)
                ],
                axis=0,
            )
            mixed = jnp.dot(w_rows[...], stacked, preferred_element_type=F32)
            for side in range(2):
                part = mixed[:, side * lanes : (side + 1) * lanes]
                outs.append(
                    part[32:64] + lane_shift(part[0:32], -1) + lane_shift(part[64:96], 1)
                )
        gi_own[:, z] = jnp.swapaxes(jnp.stack(outs), 0, 1).astype(BF16)

    for z in range(1, planes - 1):
        inputs_plane(z)

    def add_up(buffer, part, count):
        total = buffer[piece(part, 0, count)]
        for index in range(1, count):
            total = total + buffer[piece(part, index, count)]
        return total

    for part in range(3):
        first[piece(part, own[part])] = partial[piece(part, own[part])]
        whole(first, (members - 1) * units[part], recv_sem.at[0, part])
        axis = (part + 1) % 3
        mine = piece(part, place[axis], n)
        second[mine] = add_up(first, part, members)

        def spread(step, part=part, axis=axis, mine=mine):
            copy(second.at[mine], second.at[mine], 1, part, narrow(axis, step)[1]).start()

        far_out(half, spread)


    for part in range(3):
        whole(second, (n - 1) * units[part], recv_sem.at[1, part])
        axis = (part + 2) % 3
        mine = piece(part, place[axis], n)
        third[mine] = add_up(second, part, n)

        def spread(step, part=part, axis=axis, mine=mine):
            copy(third.at[mine], third.at[mine], 2, part, narrow(axis, step)[1]).start()

        far_out(half, spread)

    for part in range(3):
        whole(first, (members - 1) * units[part], send_sem.at[0, part])

    keep_own = [
        pltpu.make_async_copy(
            result.at[piece(part, own[part])],
            final_hbm.at[piece(part, own[part])],
            keep_sem.at[part],
        )
        for part in range(3)
    ]

    for part in range(3):
        whole(third, (n - 1) * units[part], recv_sem.at[2, part])
        mine = piece(part, own[part])
        result[mine] = add_up(third, part, n) * factor
        keep_own[part].start()

        def spread(step, part=part, mine=mine):
            copy(result.at[mine], final_hbm.at[mine], 3, part, wide(part, step)[1]).start()

        far_out(n, spread)

    halo_arrive(g_pair, g_halo)
    pad_plane(0, g_halo[0])
    pad_plane(planes + 1, g_halo[1])
    inputs_plane(0)
    inputs_plane(planes - 1)
    save_gi = pltpu.make_async_copy(gi_own, gi_hbm, keep_sem.at[3])
    save_gi.start()

    for part in range(3):
        whole(final_hbm, (members - 1) * units[part], recv_sem.at[3, part])

    for part in range(3):
        keep_own[part].wait()
    save_gi.wait()
    whole(g_own, chans - share, swap_sem.at[0])
    halo_sent(a_pair)
    halo_sent(g_pair)
    for part in range(3):
        whole(second, (n - 1) * units[part], send_sem.at[1, part])
        whole(third, (n - 1) * units[part], send_sem.at[2, part])
        whole(first, (members - 1) * units[part], send_sem.at[3, part])


def local(activations, grad_out, weight):
    slabs, samples = lax.axis_size("slab"), lax.axis_size("sample")
    n = slabs // 2
    _, in_chan, planes, rows, lanes = activations.shape
    chans = weight.shape[1]
    cells = samples * slabs * planes * rows * lanes
    vmem = pl.BlockSpec(memory_space=pltpu.VMEM)
    hbm = pl.BlockSpec(memory_space=pltpu.HBM)
    weight = weight.transpose(0, 2, 1)
    grad_in, packed = pl.pallas_call(
        functools.partial(fused_kernel, n, 1.0 / math.sqrt(cells)),
        out_shape=(
            jax.ShapeDtypeStruct(activations.shape[1:], BF16),
            jax.ShapeDtypeStruct((112, 4, 128), F32),
        ),
        in_specs=[hbm] * 3,
        out_specs=(hbm, hbm),
        scratch_shapes=[
            pltpu.VMEM((in_chan, planes, rows, lanes), BF16),
            pltpu.VMEM((2, in_chan, rows, lanes), BF16),
            pltpu.VMEM((chans, planes, rows, lanes), BF16),
            pltpu.VMEM((2, chans, rows, lanes), BF16),
            pltpu.VMEM(weight.shape, BF16),
            pltpu.VMEM((planes + 2, rows + 2, chans, lanes), BF16),
            pltpu.VMEM((planes + 2, rows, 128, lanes), BF16),
            pltpu.VMEM((96, 9 * chans), BF16),
            pltpu.VMEM((304, 256), F32),
            pltpu.VMEM((448, 128), F32),
            pltpu.VMEM((112, 4, 128), F32),
            pltpu.VMEM((56, 4, 128), F32),
            pltpu.VMEM((56, 4, 128), F32),
            pltpu.VMEM((112, 4, 128), F32),
            pltpu.VMEM((112, 4, 128), F32),
            pltpu.VMEM(activations.shape[1:], BF16),
            pltpu.SemaphoreType.DMA((3,)),
            pltpu.SemaphoreType.DMA((4,)),
            pltpu.SemaphoreType.DMA((2,)),
            pltpu.SemaphoreType.DMA((2, 2)),
            pltpu.SemaphoreType.DMA((2, 2)),
            pltpu.SemaphoreType.DMA((4, 3)),
            pltpu.SemaphoreType.DMA((4, 3)),
        ],
        compiler_params=pltpu.CompilerParams(
            collective_id=0, has_side_effects=True, vmem_limit_bytes=58 << 20
        ),
        name="backward",
    )(activations[0], grad_out[0], weight)
    grad_in, gw, gb = pl.pallas_call(
        unpack_kernel,
        out_shape=(
            jax.ShapeDtypeStruct(activations.shape[1:], BF16),
            jax.ShapeDtypeStruct(weight.shape, F32),
            jax.ShapeDtypeStruct((1, chans), F32),
        ),
        in_specs=[vmem, vmem],
        out_specs=(vmem, vmem, vmem),
        scratch_shapes=[pltpu.VMEM((448, 128), F32)],
        name="unpack",
    )(grad_in, packed)
    return grad_in[None], gw.transpose(0, 2, 1), gb[0]


def solution(mesh):
    placed = (P("sample", None, "slab", None, None), P("sample", "slab", None, None, None), P())
    return jax.shard_map(
        local,
        mesh=mesh,
        in_specs=placed,
        out_specs=(P("sample", None, "slab", None, None), P(), P()),
        check_vma=False,
    )
```

```python
import functools
import math

import jax
import jax.numpy as jnp
from jax import lax
from jax.experimental import pallas as pl
from jax.experimental.pallas import tpu as pltpu
from jax.sharding import PartitionSpec as P

MESH = pl.DeviceIdType.MESH
F32 = jnp.float32
BF16 = jnp.bfloat16


def lane_shift(value, shift):
    lane = lax.broadcasted_iota(jnp.int32, value.shape, value.ndim - 1)
    rolled = pltpu.roll(value, shift % 128, value.ndim - 1)
    edge = 0 if shift > 0 else 127
    return jnp.where(lane == edge, 0.0, rolled)


def far_out(middle, send):
    send(middle)

    @pl.loop(1, middle)
    def _(step):
        send(middle + step)
        send(middle - step)


def unpack_kernel(gi_hbm, final, gi_out, gw_ref, gb_ref, flat):
    gi_out[...] = gi_hbm[...]
    for block in range(112):
        flat[block * 4 : block * 4 + 4] = final[block]
    for spot, dz in enumerate((0, 2, 1)):
        for dx in range(3):
            start = spot * 96 + dx * 32
            for dy in range(2):
                gw_ref[9 * dz + 3 * dy + dx] = flat[start : start + 32, dy * 64 : dy * 64 + 64]
            for row in (start, start + 16):
                lane, line = (row // 144) * 64, 288 + row % 144
                gw_ref[9 * dz + 6 + dx, row - start : row - start + 16] = flat[
                    line : line + 16, lane : lane + 64
                ]
    gb_ref[...] = flat[432:433, 64:128]


def fused_kernel(
    n,
    factor,
    a_hbm,
    g_hbm,
    w_hbm,
    gi_hbm,
    final_hbm,
    a_own,
    a_halo,
    g_own,
    g_halo,
    w_own,
    g_pad,
    a_stack,
    w_rows,
    acc,
    flat,
    first,
    second,
    third,
    partial,
    result,
    gi_own,
    load_sem,
    keep_sem,
    swap_sem,
    halo_send,
    halo_recv,
    send_sem,
    recv_sem,
):
    in_chan, planes, rows, lanes = a_own.shape
    chans = g_own.shape[0]
    slabs = 2 * n
    share = chans // slabs
    half = n // 2
    members = 2 * n
    scale = first.shape[0] // (7 * members)
    units = (3 * scale, 2 * scale, 2 * scale)
    base = (0, 3 * scale, 5 * scale)
    slab, sample = lax.axis_index("slab"), lax.axis_index("sample")
    core = lax.rem(sample, 2)
    place = (
        lax.div(slab, n) * half + lax.rem(lax.div(sample, 2), half),
        lax.rem(slab, n),
        lax.div(sample, n),
    )
    own = [place[part] * 2 + core for part in range(3)]

    def device(axis, coordinate, other):
        x, y, z = (coordinate if axis == i else place[i] for i in range(3))
        return {
            "slab": lax.div(x, half) * n + y,
            "sample": z * n + lax.rem(x, half) * 2 + other,
        }

    def wide(axis, step):
        index = lax.rem(own[axis] + step, members)
        return index, device(axis, lax.div(index, 2), lax.rem(index, 2))

    def narrow(axis, step):
        index = lax.rem(place[axis] + step, n)
        return index, device(axis, index, core)

    load_a = pltpu.make_async_copy(a_hbm, a_own, load_sem.at[0])
    load_w = pltpu.make_async_copy(w_hbm, w_own, load_sem.at[1])
    load_g = pltpu.make_async_copy(
        g_hbm.at[:, pl.ds(slab * planes, planes)],
        g_own.at[pl.ds(slab * share, share)],
        load_sem.at[2],
    )

    barrier = pltpu.get_barrier_semaphore()

    column, side = lax.rem(slab, n), lax.div(slab, n)

    def other_slab(cross, step):
        return lax.rem(side + cross, 2) * n + lax.rem(column + step, n)

    def greet(peer):
        pl.semaphore_signal(barrier, inc=1, device_id=peer, device_id_type=MESH)

    def greet_step(step):
        greet({"slab": other_slab(1, step)})
        for axis in range(3):
            index = lax.rem(place[axis] + step, n)
            greet(device(axis, index, core))
            greet(device(axis, index, 1 - core))

    far_out(half, greet_step)

    greet(device(0, place[0], 1 - core))
    load_a.start()
    load_w.start()
    load_g.start()
    pl.semaphore_wait(barrier, 7 * (n - 1) + 1)

    def whole(buffer, count, sem):
        view = buffer.at[pl.ds(0, count)]
        pltpu.make_async_copy(view, view, sem).wait()

    def swap(cross, step):
        target = other_slab(cross, step)
        pltpu.make_async_remote_copy(
            src_ref=g_hbm.at[:, pl.ds(target * planes, planes)],
            dst_ref=g_own.at[pl.ds(slab * share, share)],
            send_sem=swap_sem.at[0],
            recv_sem=swap_sem.at[1],
            device_id={"slab": target},
            device_id_type=MESH,
        ).start()

    def halo_copy(source, target, which, side, peer):
        return pltpu.make_async_remote_copy(
            src_ref=source,
            dst_ref=target,
            send_sem=halo_send.at[which, side],
            recv_sem=halo_recv.at[which, side],
            device_id={"slab": peer},
            device_id_type=MESH,
        )

    def halo_pair(source, target, which):
        up = halo_copy(source.at[:, planes - 1], target.at[0], which, 0, lax.rem(slab + 1, slabs))
        down = halo_copy(source.at[:, 0], target.at[1], which, 1, lax.rem(slab + slabs - 1, slabs))
        return up, down

    def halo_start(pair):
        pl.when(slab < slabs - 1)(pair[0].start)
        pl.when(slab > 0)(pair[1].start)

    def halo_arrive(pair, target):
        @pl.when(slab > 0)
        def _():
            pair[0].wait_recv()

        @pl.when(slab == 0)
        def _():
            target[0] = jnp.zeros(target.shape[1:], target.dtype)

        @pl.when(slab < slabs - 1)
        def _():
            pair[1].wait_recv()

        @pl.when(slab == slabs - 1)
        def _():
            target[1] = jnp.zeros(target.shape[1:], target.dtype)

    def halo_sent(pair):
        pl.when(slab < slabs - 1)(pair[0].wait_send)
        pl.when(slab > 0)(pair[1].wait_send)

    far_first = sorted(range(n), key=lambda step: -min(step, n - step))
    for step in far_first:
        swap(1, step)
        if step:
            swap(0, step)
    load_a.wait()
    a_pair = halo_pair(a_own, a_halo, 0)
    halo_start(a_pair)

    for z in range(planes + 2):
        g_pad[z, 0] = jnp.zeros((chans, lanes), BF16)
        g_pad[z, rows + 1] = jnp.zeros((chans, lanes), BF16)

    tail = lax.broadcasted_iota(jnp.int32, (rows, 32, lanes), 1) == 0

    def stack_plane(z, plane):
        cells = jnp.swapaxes(plane.astype(F32), 0, 1)
        stack = [lane_shift(cells, 1), cells, lane_shift(cells, -1), jnp.where(tail, 1.0, 0.0)]
        for part, value in enumerate(stack):
            a_stack[z, :, part * 32 : part * 32 + 32] = value.astype(BF16)

    def pad_plane(z, plane):
        g_pad[z, 1 : rows + 1] = jnp.swapaxes(plane.astype(F32), 0, 1).astype(BF16)

    for z in range(planes):
        stack_plane(z + 1, a_own[:, z])
    load_w.wait()
    for zy in range(9):
        for dx in range(3):
            w_rows[dx * 32 : dx * 32 + 32, zy * chans : (zy + 1) * chans] = w_own[3 * zy + dx]
    halo_arrive(a_pair, a_halo)
    stack_plane(0, a_halo[0])
    stack_plane(planes + 1, a_halo[1])

    load_g.wait()
    whole(g_own, chans - share, swap_sem.at[1])
    g_pair = halo_pair(g_own, g_halo, 1)
    for z in range(planes):
        pad_plane(z + 1, g_own[:, z])

    total = None
    for z in range(planes):
        cot = jnp.concatenate(
            [
                jnp.concatenate([g_pad[z + 1, y + 1 - dy] for y in range(rows)], axis=1)
                for dy in (-1, 0, 1)
            ],
            axis=0,
        )
        cells = jnp.concatenate(
            [
                jnp.concatenate([a_stack[z + 1 + dz, y, :height] for y in range(rows)], axis=1)
                for dz, height in ((-1, 96), (1, 96), (0, 112))
            ],
            axis=0,
        )
        term = lax.dot_general(
            cells, cot, (((1,), (1,)), ((), ())), preferred_element_type=F32
        )
        if z == 0:
            acc[:, 0:192] = term
        else:
            acc[:, 0:192] += term
    low = lax.broadcasted_iota(jnp.int32, (144, 128), 1) < 64
    flat[0:144] = jnp.where(low, acc[0:144, 128:256], pltpu.roll(acc[144:288, 128:256], 64, 1))
    for block in range(112):
        if block < 72:
            partial[block] = acc[block * 4 : block * 4 + 4, 0:128]
        elif block < 108:
            partial[block] = flat[block * 4 - 288 : block * 4 - 284]
        else:
            partial[block] = acc[block * 4 - 144 : block * 4 - 140, 0:128]

    def copy(source, target, phase, part, peer):
        return pltpu.make_async_remote_copy(
            src_ref=source,
            dst_ref=target,
            send_sem=send_sem.at[phase, part],
            recv_sem=recv_sem.at[phase, part],
            device_id=peer,
            device_id_type=MESH,
        )

    def piece(part, index, count=members):
        return pl.ds(base[part] * count + index * units[part], units[part])

    def scatter(step):
        for part in range(3):
            index, peer = wide(part, step)
            copy(
                partial.at[piece(part, index)], first.at[piece(part, own[part])], 0, part, peer
            ).start()

    far_out(n, scatter)
    halo_start(g_pair)

    def inputs_plane(z):
        outs = []
        for y in range(0, rows, 2):
            stacked = jnp.concatenate(
                [
                    jnp.concatenate(
                        [g_pad[z + 1 - dz, y + 1 - dy], g_pad[z + 1 - dz, y + 2 - dy]], axis=1
                    )
                    for dz in (-1, 0, 1)
                    for dy in (-1, 0, 1)
                ],
                axis=0,
            )
            mixed = jnp.dot(w_rows[...], stacked, preferred_element_type=F32)
            for side in range(2):
                part = mixed[:, side * lanes : (side + 1) * lanes]
                outs.append(
                    part[32:64] + lane_shift(part[0:32], -1) + lane_shift(part[64:96], 1)
                )
        gi_own[:, z] = jnp.swapaxes(jnp.stack(outs), 0, 1).astype(BF16)

    for z in range(1, planes - 1):
        inputs_plane(z)

    def add_up(buffer, part, count):
        total = buffer[piece(part, 0, count)]
        for index in range(1, count):
            total = total + buffer[piece(part, index, count)]
        return total

    for part in range(3):
        first[piece(part, own[part])] = partial[piece(part, own[part])]
        whole(first, (members - 1) * units[part], recv_sem.at[0, part])
        axis = (part + 1) % 3
        mine = piece(part, place[axis], n)
        second[mine] = add_up(first, part, members)

        def spread(step, part=part, axis=axis, mine=mine):
            copy(second.at[mine], second.at[mine], 1, part, narrow(axis, step)[1]).start()

        far_out(half, spread)


    for part in range(3):
        whole(second, (n - 1) * units[part], recv_sem.at[1, part])
        axis = (part + 2) % 3
        mine = piece(part, place[axis], n)
        third[mine] = add_up(second, part, n)

        def spread(step, part=part, axis=axis, mine=mine):
            copy(third.at[mine], third.at[mine], 2, part, narrow(axis, step)[1]).start()

        far_out(half, spread)

    for part in range(3):
        whole(first, (members - 1) * units[part], send_sem.at[0, part])

    keep_own = [
        pltpu.make_async_copy(
            result.at[piece(part, own[part])],
            final_hbm.at[piece(part, own[part])],
            keep_sem.at[part],
        )
        for part in range(3)
    ]

    for part in range(3):
        whole(third, (n - 1) * units[part], recv_sem.at[2, part])
        mine = piece(part, own[part])
        result[mine] = add_up(third, part, n) * factor
        keep_own[part].start()

        def spread(step, part=part, mine=mine):
            copy(result.at[mine], final_hbm.at[mine], 3, part, wide(part, step)[1]).start()

        far_out(n, spread)

    halo_arrive(g_pair, g_halo)
    pad_plane(0, g_halo[0])
    pad_plane(planes + 1, g_halo[1])
    inputs_plane(0)
    inputs_plane(planes - 1)
    save_gi = pltpu.make_async_copy(gi_own, gi_hbm, keep_sem.at[3])
    save_gi.start()

    for part in range(3):
        whole(final_hbm, (members - 1) * units[part], recv_sem.at[3, part])

    for part in range(3):
        keep_own[part].wait()
    save_gi.wait()
    whole(g_own, chans - share, swap_sem.at[0])
    halo_sent(a_pair)
    halo_sent(g_pair)
    for part in range(3):
        whole(second, (n - 1) * units[part], send_sem.at[1, part])
        whole(third, (n - 1) * units[part], send_sem.at[2, part])
        whole(first, (members - 1) * units[part], send_sem.at[3, part])


def local(activations, grad_out, weight):
    slabs, samples = lax.axis_size("slab"), lax.axis_size("sample")
    n = slabs // 2
    _, in_chan, planes, rows, lanes = activations.shape
    chans = weight.shape[1]
    cells = samples * slabs * planes * rows * lanes
    vmem = pl.BlockSpec(memory_space=pltpu.VMEM)
    hbm = pl.BlockSpec(memory_space=pltpu.HBM)
    weight = weight.transpose(0, 2, 1)
    grad_in, packed = pl.pallas_call(
        functools.partial(fused_kernel, n, 1.0 / math.sqrt(cells)),
        out_shape=(
            jax.ShapeDtypeStruct(activations.shape[1:], BF16),
            jax.ShapeDtypeStruct((112, 4, 128), F32),
        ),
        in_specs=[hbm] * 3,
        out_specs=(hbm, hbm),
        scratch_shapes=[
            pltpu.VMEM((in_chan, planes, rows, lanes), BF16),
            pltpu.VMEM((2, in_chan, rows, lanes), BF16),
            pltpu.VMEM((chans, planes, rows, lanes), BF16),
            pltpu.VMEM((2, chans, rows, lanes), BF16),
            pltpu.VMEM(weight.shape, BF16),
            pltpu.VMEM((planes + 2, rows + 2, chans, lanes), BF16),
            pltpu.VMEM((planes + 2, rows, 128, lanes), BF16),
            pltpu.VMEM((96, 9 * chans), BF16),
            pltpu.VMEM((304, 256), F32),
            pltpu.VMEM((448, 128), F32),
            pltpu.VMEM((112, 4, 128), F32),
            pltpu.VMEM((56, 4, 128), F32),
            pltpu.VMEM((56, 4, 128), F32),
            pltpu.VMEM((112, 4, 128), F32),
            pltpu.VMEM((112, 4, 128), F32),
            pltpu.VMEM(activations.shape[1:], BF16),
            pltpu.SemaphoreType.DMA((3,)),
            pltpu.SemaphoreType.DMA((4,)),
            pltpu.SemaphoreType.DMA((2,)),
            pltpu.SemaphoreType.DMA((2, 2)),
            pltpu.SemaphoreType.DMA((2, 2)),
            pltpu.SemaphoreType.DMA((4, 3)),
            pltpu.SemaphoreType.DMA((4, 3)),
        ],
        compiler_params=pltpu.CompilerParams(
            collective_id=0, has_side_effects=True, vmem_limit_bytes=58 << 20
        ),
        name="backward",
    )(activations[0], grad_out[0], weight)
    grad_in, gw, gb = pl.pallas_call(
        unpack_kernel,
        out_shape=(
            jax.ShapeDtypeStruct(activations.shape[1:], BF16),
            jax.ShapeDtypeStruct(weight.shape, F32),
            jax.ShapeDtypeStruct((1, chans), F32),
        ),
        in_specs=[vmem, vmem],
        out_specs=(vmem, vmem, vmem),
        scratch_shapes=[pltpu.VMEM((448, 128), F32)],
        name="unpack",
    )(grad_in, packed)
    return grad_in[None], gw.transpose(0, 2, 1), gb[0]


def solution(mesh):
    placed = (P("sample", None, "slab", None, None), P("sample", "slab", None, None, None), P())
    return jax.shard_map(
        local,
        mesh=mesh,
        in_specs=placed,
        out_specs=(P("sample", None, "slab", None, None), P(), P()),
        check_vma=False,
    )
```
